32 devices in a mesh: grp: 2 (over y), keys: 4 (over x, core), qry: 4 (over z).
Axes of the slice: x: 2, y: 2, z: 4, core: 2. Of those that a mesh axis runs over, the one named last changes fastest.
Arguments:
- queries: bfloat16 [4096, 8, 128], P(('grp', 'keys', 'qry')), parts along dimension 0, may hold values from -40 to 40, as said below
- cache_keys: bfloat16 [4096, 128], P(('grp', 'keys')), parts along dimension 0, may hold values from -128 to 128, as said below
- cache_values: bfloat16 [4096, 128], P(('grp', 'keys')), parts along dimension 0, may hold values from -24 to 24
- entry: int32 [8, 4], P(('grp', 'keys'), 'qry'), parts along dimension 0, may hold values from 0 to 3
- visits: int32 [8, 4], P(('grp', 'keys'), 'qry'), parts along dimension 0, may hold values from 3 to 4
- doc_length: int32 [2], P('grp'), parts along dimension 0, may hold values from 1025 to 2048
- slot_params: float32 [2048, 256], P(('grp', 'keys', 'qry')), parts along dimension 0, may hold values from -128 to 128, as said below
- first_moment: float32 [2048, 256], P(('grp', 'keys', 'qry')), parts along dimension 0, may hold values from -3 to 3
- second_moment: float32 [2048, 256], P(('grp', 'keys', 'qry')), parts along dimension 0, may hold values from 0.05 to 1
Outputs:
- teacher_out: bfloat16 [4096, 8, 128], P(('grp', 'keys', 'qry')), parts along dimension 0
- slot_grad: float32 [2048, 256], P(('grp', 'keys', 'qry')), parts along dimension 0
- new_params: float32 [2048, 256], P(('grp', 'keys', 'qry')), parts along dimension 0
- new_first: float32 [2048, 256], P(('grp', 'keys', 'qry')), parts along dimension 0
- new_second: float32 [2048, 256], P(('grp', 'keys', 'qry')), parts along dimension 0
- loss: float32 [2], P('grp'), parts along dimension 0
The draws below stay inside these ranges and needn't reach their ends.
There are 2 independent parts, one for each index of `grp`. The reference program is written for one: setup_inputs(seed, part) draws one part's arguments, and reference() takes and returns one part's arrays. A program takes and returns all parts, laid end to end along the dimension named above; each array names one. Nothing has to cross between parts.
Inputs may be any that keep to these rules, and one draw needn't show every extreme that they name: `queries`: query entries stay within the stated range. `cache_keys`: cache key entries stay within the stated range. `slot_params`: slot entries stay within the stated range.
All inputs are finite; a program needn't handle non-finite values.
Results may differ from the reference program's by a relative error of at most 0.0045.
Values may be sent and summed in bfloat16 or wider, within the bound.
No kernel may reach another device: no remote copies, remote signals or barrier semaphores. Data moves between devices by JAX's collectives and lax.ppermute only.
A program may use at most 64 MiB of HBM per device.

```python
import math
import jax
import jax.numpy as jnp
from jax import lax

HEADS = 8
HEAD_SIZE = 128
SLOTS = 1024
TOK_DEV = 128
CACHE_DEV = 512
TOKENS = 2048
CACHE = 2048
NBLK = 16
VMIN = 3
N_KEYS = 4
N_QRY = 4


def draw_queries(key, part):
    shape = (TOKENS, HEADS, HEAD_SIZE)
    base = jnp.clip(jax.random.normal(key, shape, jnp.float32), -6.0, 6.0)
    return base.astype(jnp.bfloat16)


def draw_cache_keys(key, part):
    shape = (CACHE, HEAD_SIZE)
    base = jnp.clip(2.0 * jax.random.normal(key, shape, jnp.float32), -12.0, 12.0)
    return base.astype(jnp.bfloat16)


def draw_slot_params(key, part):
    shape = (SLOTS, 2 * HEAD_SIZE)
    base = jnp.clip(jax.random.normal(key, shape, jnp.float32), -6.0, 6.0)
    return base


def touch_ends(drawn, rng, low, top_value):
    spot = [jax.random.randint(jax.random.fold_in(rng, axis), (), 0, length) for axis, length in enumerate(drawn.shape)]
    longest = drawn.shape.index(max(drawn.shape))
    next_to = spot[:longest] + [(spot[longest] + 1) % drawn.shape[longest]] + spot[longest + 1:]
    return drawn.at[tuple(spot)].set(low).at[tuple(next_to)].set(top_value)


def block_levels(stream_key, extent, pieces, low, largest):
    factor_of, own = 1.0, jax.random.fold_in(stream_key, 6)
    for axis_at, shards_of in pieces:
        draws = jnp.exp(jax.random.uniform(jax.random.fold_in(own, axis_at), (shards_of,), jnp.float32, low / len(pieces), largest / len(pieces)))
        factor_of = factor_of * jnp.repeat(draws, extent[axis_at] // shards_of).reshape([-1 if axis == axis_at else 1 for axis in range(len(extent))])
    return factor_of


def bell_draw(key, dims, deviation, most, split=(), kind=jnp.bfloat16):
    entries = jax.random.normal(key, dims, jnp.float32) * deviation
    if len(split) > 0:
        entries = block_levels(key, dims, split, -0.22, 0.18) * entries
    return jnp.clip(entries, min=-most, max=most).astype(kind)


def setup_inputs(seed: int = 0, part: int = 0) -> dict:
    arg_keys = jax.random.split(jax.random.key(seed), 10)
    part_keys = jax.random.split(jax.random.fold_in(arg_keys[9], part), 10)
    queries = draw_queries(jax.random.fold_in(jax.random.fold_in(arg_keys[9], part), 71), part)
    cache_keys = draw_cache_keys(jax.random.fold_in(jax.random.fold_in(arg_keys[9], part), 71), part)
    cache_values = bell_draw(part_keys[2], (CACHE, HEAD_SIZE), 4.0, 24.0, ((0, 4),))
    entry = touch_ends(jax.random.randint(part_keys[3], (N_KEYS, N_QRY), 0, N_KEYS), jax.random.fold_in(part_keys[3], 1), 0, N_KEYS - 1).astype(jnp.int32)
    visits = touch_ends(jax.random.randint(part_keys[4], (N_KEYS, N_QRY), VMIN, N_KEYS + 1), jax.random.fold_in(part_keys[4], 1), VMIN, N_KEYS).astype(jnp.int32)
    doc_length = jax.random.randint(part_keys[5], (1,), CACHE // 2 + 1, CACHE + 1).astype(jnp.int32)
    slot_params = draw_slot_params(jax.random.fold_in(jax.random.fold_in(arg_keys[9], part), 71), part)
    first_moment = bell_draw(part_keys[7], (SLOTS, 2 * HEAD_SIZE), 0.5, 3.0, ((0, 16),), jnp.float32)
    second_moment = jnp.clip(jnp.exp(math.log(1.0) - 2.9957323 * jax.random.uniform(part_keys[8], (SLOTS, 2 * HEAD_SIZE), jnp.float32) ** block_levels(part_keys[8], (SLOTS, 2 * HEAD_SIZE), ((0, 16),), -0.2, 0.2)), 0.05, 1.0)
    return dict(queries=queries, cache_keys=cache_keys, cache_values=cache_values, entry=entry, visits=visits, doc_length=doc_length, slot_params=slot_params, first_moment=first_moment, second_moment=second_moment)


NEG = -1e+30

def row_scores(left, right):
    return lax.dot_general(left, right, (((1,), (1,)), ((), ())), preferred_element_type=jnp.float32)

def student_tile(loop_state, block_entry, student_keys, student_values, score_scale):
    key_gradient, squared_terms = loop_state
    query_portion, target = block_entry
    logit_score = row_scores(query_portion, student_keys) * score_scale
    peak = lax.optimization_barrier(jnp.max(logit_score, axis=1, keepdims=True))
    weight = jnp.exp(logit_score - peak)
    prob = weight / lax.optimization_barrier(jnp.sum(weight, axis=1, keepdims=True))
    block_prob = prob.astype(jnp.bfloat16)
    student_output = jnp.dot(block_prob, student_values, preferred_element_type=jnp.float32)
    diff = student_output - target.astype(jnp.float32)
    squared_terms = squared_terms + jnp.sum(diff * diff)
    block_difference = diff.astype(jnp.bfloat16)
    prob_gradient = row_scores(block_difference, student_values)
    inner = lax.optimization_barrier(jnp.sum(prob * prob_gradient, axis=1, keepdims=True))
    dscore = (prob * (prob_gradient - inner) * score_scale).astype(jnp.bfloat16)
    dkeys = lax.dot_general(dscore, query_portion, (((0,), (0,)), ((), ())), preferred_element_type=jnp.float32)
    dvals = lax.dot_general(block_prob, block_difference, (((0,), (0,)), ((), ())), preferred_element_type=jnp.float32)
    key_gradient = key_gradient + jnp.concatenate([dkeys, dvals], axis=1)
    return ((key_gradient, squared_terms), None)

def reference(queries, cache_keys, cache_values, entry, visits, doc_length, slot_params, first_moment, second_moment):
    score_scale = 1.0 / math.sqrt(HEAD_SIZE)
    flat_entry = entry.reshape(-1)
    flat_visits = visits.reshape(-1)
    length = doc_length[0]

    def teacher_block(index):
        kidx = index // N_QRY
        start = flat_entry[index]
        count = flat_visits[index]
        query_portion = lax.dynamic_slice_in_dim(queries, (index * TOK_DEV).astype(jnp.int32), TOK_DEV, 0).reshape(TOK_DEV * HEADS, HEAD_SIZE)
        logit_score = row_scores(query_portion, cache_keys) * score_scale
        place = lax.iota(jnp.int32, CACHE)
        shard = place // CACHE_DEV
        live = (jnp.remainder(shard - kidx - start, N_KEYS) < count) & (place < length)
        live = live[None, :]
        logit_score = jnp.where(live, logit_score, NEG)
        peak = lax.optimization_barrier(jnp.max(logit_score, axis=1, keepdims=True))
        weight = jnp.where(live, jnp.exp(logit_score - peak), 0.0)
        total = lax.optimization_barrier(jnp.sum(weight, axis=1, keepdims=True))
        acc = jnp.dot(weight.astype(jnp.bfloat16), cache_values, preferred_element_type=jnp.float32)
        return (acc / total).astype(jnp.bfloat16).reshape(TOK_DEV, HEADS, HEAD_SIZE)
    teacher = lax.map(teacher_block, jnp.arange(NBLK, dtype=jnp.int32))
    teacher = teacher.reshape(TOKENS, HEADS, HEAD_SIZE)
    slot_replica = slot_params.astype(jnp.bfloat16)
    student_keys = slot_replica[:, :HEAD_SIZE]
    student_values = slot_replica[:, HEAD_SIZE:]
    rows = TOKENS * HEADS
    block = math.gcd(rows, 512)
    query_blocks = queries.reshape(rows // block, block, HEAD_SIZE)
    teacher_tiles = teacher.reshape(rows // block, block, HEAD_SIZE)
    initial_state = (jnp.zeros((SLOTS, 2 * HEAD_SIZE), jnp.float32), jnp.zeros((), jnp.float32))
    (key_gradient, squared_terms), ignored_value = lax.scan(lambda column_index, loop_index: student_tile(column_index, loop_index, student_keys, student_values, score_scale), initial_state, (query_blocks, teacher_tiles))
    new_first = 0.9 * first_moment + 0.1 * key_gradient
    new_second = 0.95 * second_moment + 0.05 * key_gradient * key_gradient
    new_params = slot_params - 0.02 * new_first / (jnp.sqrt(new_second) + 1e-08)
    loss = (squared_terms / rows).reshape(1)
    return (teacher, key_gradient, new_params, new_first, new_second, loss)
```

```python
import math

import jax
import jax.numpy as jnp
from jax import lax
from jax.experimental import pallas as pl
from jax.experimental.pallas import tpu as pltpu
from jax.sharding import PartitionSpec as P

NEG = -1e30
PAD = 8
LANES = 128
GRANT = 24 * 2**20


def nt(left, right):
    return lax.dot_general(left, right, (((1,), (1,)), ((), ())), preferred_element_type=jnp.float32)


def nn(left, right):
    return jnp.dot(left, right, preferred_element_type=jnp.float32)


def with_ones(values):
    turned = values.T
    return jnp.concatenate([turned, jnp.ones((PAD, turned.shape[1]), turned.dtype)], axis=0)


def row_block(rows):
    return math.gcd(rows, 256)


def call(kernel, name, out, scalars, arrays, scratch=(), hbm_out=()):
    vm = pl.BlockSpec(memory_space=pltpu.VMEM)
    sm = pl.BlockSpec(memory_space=pltpu.SMEM)
    arrays = [pltpu.with_memory_space_constraint(a, pltpu.VMEM) for a in arrays]
    shapes = tuple(
        jax.ShapeDtypeStruct(s, d) if i in hbm_out else pltpu.VMEM(s, d) for i, (s, d) in enumerate(out)
    )
    return pl.pallas_call(
        kernel,
        out_shape=shapes,
        in_specs=[sm] * len(scalars) + [vm] * len(arrays),
        out_specs=tuple(vm for _ in shapes),
        scratch_shapes=list(scratch),
        compiler_params=pltpu.CompilerParams(vmem_limit_bytes=GRANT),
        name=name,
    )(*scalars, *arrays)


def teacher(scalars, queries, segments, state, last, scale):
    rows, width = queries.shape
    step = row_block(rows)
    shapes = [((1, rows), jnp.float32), ((width + PAD, rows), jnp.float32)]
    ends = [((rows, width), jnp.bfloat16), ((width, rows), jnp.bfloat16)]
    offsets = [j for j, _ in segments]
    first = state is None
    factor = scale * math.log2(math.e)

    def kernel(entry_ref, visits_ref, length_ref, q_ref, *refs):
        seg, refs = refs[: 2 * len(offsets)], refs[2 * len(offsets):]
        if not first:
            (big_in, acc_in), refs = refs[:2], refs[2:]
        if last:
            (out_ref, outt_ref), refs = refs[:2], refs[2:]
        big_ref, acc_ref = refs
        me = lax.axis_index("keys")
        n_keys = lax.axis_size("keys")
        if first:
            big_ref[...] = jnp.full(big_ref.shape, NEG, jnp.float32)
            acc_ref[...] = jnp.zeros(acc_ref.shape, jnp.float32)
        else:
            big_ref[...] = big_in[...]
            acc_ref[...] = acc_in[...]
        for s, offset in enumerate(offsets):
            keys_ref, values_ref = seg[2 * s], seg[2 * s + 1]
            shard = me ^ offset
            size = keys_ref.shape[0]
            turn = lax.rem(shard - me - entry_ref[0, 0] + 2 * n_keys, n_keys)
            left = jnp.clip(length_ref[0] - shard * size, 0, size)
            count = jnp.where(turn < visits_ref[0, 0], left, 0)

            @pl.when(count > 0)
            def _():
                keys = keys_ref[...]
                turned = with_ones(values_ref[...])
                live = lax.broadcasted_iota(jnp.int32, (size, 1), 0) < count

                def one(at):
                    score = jnp.where(live, nt(keys, q_ref[pl.ds(at, step), :]), NEG)
                    big = big_ref[:, pl.ds(at, step)]
                    new_big = jnp.maximum(big, jnp.max(score, axis=0, keepdims=True))
                    weight = jnp.exp2((score - new_big) * factor).astype(jnp.bfloat16)
                    fade = jnp.exp2((big - new_big) * factor)
                    acc_ref[:, pl.ds(at, step)] = acc_ref[:, pl.ds(at, step)] * fade + nn(turned, weight)
                    big_ref[:, pl.ds(at, step)] = new_big

                if len(offsets) <= 4:
                    for i in range(rows // step):
                        one(i * step)
                else:
                    pl.loop(0, rows // step)(lambda i: one(pl.multiple_of(i * step, step)))

        if last:
            for i in range(rows // step):
                at = i * step
                total = acc_ref[width:width + 1, pl.ds(at, step)]
                done = (acc_ref[:width, pl.ds(at, step)] / total).astype(jnp.bfloat16)
                outt_ref[:, pl.ds(at, step)] = done
                out_ref[pl.ds(at, step), :] = done.T

    arrays = [queries] + [a for _, pair in segments for a in pair] + ([] if first else list(state))
    scratch = [pltpu.VMEM(s, d) for s, d in shapes] if last else []
    return call(
        kernel, "teacher_last" if last else "teacher_part", ends if last else shapes, scalars, arrays, scratch,
        hbm_out=(0,) if last else (),
    )


def gradient_half(start, half, q_ref, prob_ref, cast_ref, diff_ref, inner_ref, values_ref, grad_ref, scale):
    rows, width = q_ref.shape
    step = row_block(rows)
    values = values_ref[pl.ds(start, half), :]
    dkeys = jnp.zeros((half, width), jnp.float32)
    dvals = jnp.zeros((half, width), jnp.float32)
    for i in range(rows // step):
        at = i * step
        diff = diff_ref[pl.ds(at, step), :]
        slope = nt(values, diff) - inner_ref[:, pl.ds(at, step)]
        dscore = (prob_ref[pl.ds(start, half), pl.ds(at, step)] * slope).astype(jnp.bfloat16)
        dkeys = dkeys + nn(dscore, q_ref[pl.ds(at, step), :])
        dvals = dvals + nn(cast_ref[pl.ds(start, half), pl.ds(at, step)], diff)
    grad_ref[:, :width] = dkeys * scale
    grad_ref[:, width:] = dvals


def student(queries, teach, slots, other, per, half, scale):
    rows, width = queries.shape
    step = row_block(rows)
    pieces = slots.shape[0] // per
    count = 2 * slots.shape[0]
    factor = scale * math.log2(math.e)

    def kernel(
        q_ref, teach_ref, slots_ref, other_ref,
        grad_ref, prob_ref, cast_ref, diff_ref, inner_ref, values_ref, loss_ref, keys_ref,
    ):
        n_chip, n_qry = lax.axis_size("keys") // 2, lax.axis_size("qry")
        me, mine = lax.axis_index("keys"), lax.axis_index("qry")
        core, chip = lax.rem(me, 2), lax.div(me, 2)
        for source, c in ((slots_ref, core), (other_ref, 1 - core)):
            for j in range(pieces):
                d, x = divmod(j, n_chip)
                place = (c * n_chip + (chip ^ x)) * n_qry + lax.rem(mine - d + n_qry, n_qry)
                to = pl.multiple_of(place * per, per)
                piece = source[pl.ds(j * per, per), :]
                keys_ref[pl.ds(to, per), :] = piece[:, :width]
                values_ref[pl.ds(to, per), :] = piece[:, width:]
        turned = with_ones(values_ref[...])
        squares = jnp.zeros((width, step), jnp.float32)
        for i in range(rows // step):
            at = i * step
            score = nt(keys_ref[...], q_ref[pl.ds(at, step), :])
            big = jnp.max(score, axis=0, keepdims=True)
            weight = jnp.exp2((score - big) * factor)
            prob = weight * (1.0 / jnp.sum(weight, axis=0, keepdims=True))
            prob_ref[:, pl.ds(at, step)] = prob
            cast = prob.astype(jnp.bfloat16)
            cast_ref[:, pl.ds(at, step)] = cast
            both = nn(turned, cast)
            out, mass = both[:width, :], both[width:width + 1, :]
            diff = out - teach_ref[:, pl.ds(at, step)].astype(jnp.float32)
            squares = squares + diff * diff
            short = diff.astype(jnp.bfloat16)
            diff_ref[pl.ds(at, step), :] = short.T
            inner_ref[:, pl.ds(at, step)] = jnp.sum(short.astype(jnp.float32) * out, axis=0, keepdims=True) / mass
        loss_ref[...] = jnp.full(loss_ref.shape, jnp.sum(squares), jnp.float32)
        gradient_half(
            pl.multiple_of((1 - core) * half, half),
            half, q_ref, prob_ref, cast_ref, diff_ref, inner_ref, values_ref, grad_ref, scale,
        )

    return call(
        kernel, "student",
        [
            ((half, 2 * width), jnp.float32),
            ((count, rows), jnp.float32),
            ((count, rows), jnp.bfloat16),
            ((rows, width), jnp.bfloat16),
            ((1, rows), jnp.float32),
            ((count, width), jnp.bfloat16),
            ((PAD, LANES), jnp.float32),
        ],
        [], [queries, teach, slots, other],
        [pltpu.VMEM((count, width), jnp.bfloat16)],
    )


def own_half(queries, prob, cast, diff, inner, values, half, scale):
    def kernel(*refs):
        start = pl.multiple_of(lax.rem(lax.axis_index("keys"), 2) * half, half)
        gradient_half(start, half, *refs, scale)

    return call(
        kernel, "own_half", [((half, 2 * queries.shape[1]), jnp.float32)],
        [], [queries, prob, cast, diff, inner, values],
    )[0]


def packed(own, got, loss, heard, per):
    half, wide = own.shape
    blocks = half // per

    def kernel(own_ref, got_ref, loss_ref, heard_ref, out_ref):
        squares = loss_ref[...] + heard_ref[...]
        one = squares.astype(jnp.bfloat16)
        left = squares - one.astype(jnp.float32)
        two = left.astype(jnp.bfloat16)
        three = (left - two.astype(jnp.float32)).astype(jnp.bfloat16)
        place = lax.broadcasted_iota(jnp.int32, (PAD, LANES), 0)
        zero = jnp.zeros((PAD, LANES), jnp.float32)
        parts = jnp.where(
            place == 0, one.astype(jnp.float32),
            jnp.where(place == 1, two.astype(jnp.float32), jnp.where(place == 2, three.astype(jnp.float32), zero)),
        ).astype(jnp.bfloat16)
        for b in range(blocks):
            at = b * per
            out_ref[b, :per, :] = (own_ref[pl.ds(at, per), :] + got_ref[pl.ds(at, per), :]).astype(jnp.bfloat16)
            for at in range(0, wide, LANES):
                out_ref[b, per:, pl.ds(at, LANES)] = parts

    return call(
        kernel, "packed", [((blocks, per + PAD, wide), jnp.bfloat16)], [], [own, got, loss, heard]
    )[0]


def update(heard, slot_params, first_moment, second_moment, terms):
    per, wide = slot_params.shape

    def kernel(heard_ref, params_ref, first_ref, second_ref, grad_ref, p_ref, f_ref, s_ref, loss_ref):
        grad = jnp.zeros((per, wide), jnp.float32)
        tail = jnp.zeros((PAD, LANES), jnp.float32)
        for b in range(heard_ref.shape[0]):
            grad = grad + heard_ref[b, :per, :].astype(jnp.float32)
            tail = tail + heard_ref[b, per:, :LANES].astype(jnp.float32)
        grad_ref[...] = grad
        new_first = 0.9 * first_ref[...] + 0.1 * grad
        new_second = 0.95 * second_ref[...] + 0.05 * grad * grad
        f_ref[...] = new_first
        s_ref[...] = new_second
        p_ref[...] = params_ref[...] - 0.02 * new_first / (jnp.sqrt(new_second) + 1e-08)
        loss_ref[...] = jnp.sum(tail, axis=0, keepdims=True) / terms

    shape = ((per, wide), jnp.float32)
    return call(
        kernel, "update", [shape] * 4 + [((1, LANES), jnp.float32)], [],
        [heard, slot_params, first_moment, second_moment], hbm_out=(0, 1, 2, 3, 4),
    )


def after(value, *others):
    return lax.optimization_barrier((value,) + others)[0]


def body(
    queries,
    cache_keys,
    cache_values,
    entry,
    visits,
    doc_length,
    slot_params,
    first_moment,
    second_moment,
):
    n_keys, n_qry = lax.axis_size("keys"), lax.axis_size("qry")
    tok, heads, width = queries.shape
    rows = tok * heads
    per = slot_params.shape[0]
    n_chip = n_keys // 2
    half = n_chip * n_qry * per
    scale = 1.0 / math.sqrt(width)
    flat = queries.reshape(rows, width)
    scalars = [entry, visits, doc_length]

    def swap(block, bit):
        return lax.ppermute(block, "keys", [(k, k ^ bit) for k in range(n_keys)])

    copies = slot_params.astype(jnp.bfloat16)
    chips = {0: copies}
    low = [0] + [j & -j for j in range(1, n_keys)]
    for j in range(2, n_keys, 2):
        chips[j] = swap(chips[j ^ low[j]], low[j])

    cache = {0: (cache_keys, cache_values)}
    for j in list(range(2, n_keys, 2)) + list(range(1, n_keys, 2)):
        cache[j] = tuple(swap(a, low[j]) for a in cache[j ^ low[j]])

    state = teacher(scalars, flat, [(0, cache[0])], None, False, scale)

    column = jnp.concatenate([chips[j] for j in range(0, n_keys, 2)], axis=0)
    column = after(column, state)
    rounds = [column] + [
        lax.ppermute(column, "qry", [(i, (i + d) % n_qry) for i in range(n_qry)]) for d in range(1, n_qry)
    ]
    slots = jnp.concatenate(rounds, axis=0)
    other = swap(slots, 1)

    state = teacher(scalars, flat, [(1, cache[1])], state, False, scale)
    rest = list(range(2, n_keys, 2)) + list(range(3, n_keys, 2))
    teacher_rows, teacher_turned = teacher(scalars, flat, [(j, cache[j]) for j in rest], state, True, scale)

    away, prob, cast, diff, inner, values, loss = student(flat, teacher_turned, slots, other, per, half, scale)
    own = own_half(flat, prob, cast, diff, inner, values, half, scale)
    sent = packed(own, swap(away, 1), loss, swap(loss, 1), per)

    groups = [[(2 * x + c) * n_qry + q for x in range(n_chip) for q in range(n_qry)] for c in range(2)]
    heard = lax.all_to_all(sent, ("keys", "qry"), 0, 0, axis_index_groups=groups, tiled=True)
    slot_grad, new_params, new_first, new_second, loss = update(
        heard, slot_params, first_moment, second_moment, rows * n_keys * n_qry
    )
    teacher_out = teacher_rows.reshape(tok, heads, width)
    return (teacher_out, slot_grad, new_params, new_first, new_second, loss[0, :1])


def solution(mesh):
    return jax.shard_map(
        body,
        mesh=mesh,
        in_specs=(
            P(("grp", "keys", "qry"), None, None),
            P(("grp", "keys"), None),
            P(("grp", "keys"), None),
            P(("grp", "keys"), "qry"),
            P(("grp", "keys"), "qry"),
            P("grp"),
            P(("grp", "keys", "qry"), None),
            P(("grp", "keys", "qry"), None),
            P(("grp", "keys", "qry"), None),
        ),
        out_specs=(
            P(("grp", "keys", "qry"), None, None),
            P(("grp", "keys", "qry"), None),
            P(("grp", "keys", "qry"), None),
            P(("grp", "keys", "qry"), None),
            P(("grp", "keys", "qry"), None),
            P("grp"),
        ),
        check_vma=False,
    )
```

```python
import math

import jax
import jax.numpy as jnp
from jax import lax
from jax.experimental import pallas as pl
from jax.experimental.pallas import tpu as pltpu
from jax.sharding import PartitionSpec as P


NEG = -1e30
PAD = 8
LANES = 128
GRANT = 24 * 2**20


def nt(left, right):
    return lax.dot_general(left, right, (((1,), (1,)), ((), ())), preferred_element_type=jnp.float32)


def nn(left, right):
    return jnp.dot(left, right, preferred_element_type=jnp.float32)


def with_ones(values):
    turned = values.T
    return jnp.concatenate([turned, jnp.ones((PAD, turned.shape[1]), turned.dtype)], axis=0)


def row_block(rows):
    return math.gcd(rows, 256)


def call(kernel, out, scalars, arrays, scratch=(), hbm_out=()):
    vm = pl.BlockSpec(memory_space=pltpu.VMEM)
    sm = pl.BlockSpec(memory_space=pltpu.SMEM)
    arrays = [pltpu.with_memory_space_constraint(a, pltpu.VMEM) for a in arrays]
    shapes = tuple(
        jax.ShapeDtypeStruct(s, d) if i in hbm_out else pltpu.VMEM(s, d) for i, (s, d) in enumerate(out)
    )
    return pl.pallas_call(
        kernel,
        out_shape=shapes,
        in_specs=[sm] * len(scalars) + [vm] * len(arrays),
        out_specs=tuple(vm for _ in shapes),
        scratch_shapes=list(scratch),
        compiler_params=pltpu.CompilerParams(vmem_limit_bytes=GRANT),
    )(*scalars, *arrays)


def load(queries, keys, values, slot_params):
    size, width = keys.shape
    ins = [pltpu.with_memory_space_constraint(a, pltpu.HBM) for a in (slot_params, keys, values, queries)]

    def kernel(*refs):
        sources, (slots_ref, cache_ref, q_ref, full_ref, sems) = refs[:4], refs[4:]
        targets = (full_ref, cache_ref.at[pl.ds(0, size)], cache_ref.at[pl.ds(size, size)], q_ref)
        moves = [pltpu.make_async_copy(a, b, sems.at[i]) for i, (a, b) in enumerate(zip(sources, targets))]
        for move in moves:
            move.start()
        moves[0].wait()
        slots_ref[...] = full_ref[...].astype(jnp.bfloat16)
        for move in moves[1:]:
            move.wait()

    return pl.pallas_call(
        kernel,
        out_shape=(
            pltpu.VMEM(slot_params.shape, jnp.bfloat16),
            pltpu.VMEM((2 * size, width), keys.dtype),
            pltpu.VMEM(queries.shape, queries.dtype),
        ),
        in_specs=[pl.BlockSpec(memory_space=pltpu.HBM)] * 4,
        out_specs=(pl.BlockSpec(memory_space=pltpu.VMEM),) * 3,
        scratch_shapes=[
            pltpu.VMEM(slot_params.shape, slot_params.dtype),
            pltpu.SemaphoreType.DMA((4,)),
        ],
        compiler_params=pltpu.CompilerParams(vmem_limit_bytes=GRANT),
        name="load",
    )(*ins)


def teacher(live, queries, segments, state, last, scale):
    rows, width = queries.shape
    step = row_block(rows)
    shapes = [((1, rows), jnp.float32), ((width + PAD, rows), jnp.float32)]
    ends = [((rows, width), jnp.bfloat16), ((width, rows), jnp.bfloat16)]
    offsets = [j for j, _ in segments]
    first = state is None
    factor = scale * math.log2(math.e)

    def kernel(live_ref, q_ref, *refs):
        seg, refs = refs[: len(offsets)], refs[len(offsets):]
        if not first:
            (big_in, acc_in), refs = refs[:2], refs[2:]
        if last:
            (out_ref, outt_ref), refs = refs[:2], refs[2:]
        big_ref, acc_ref, score_ref, peak_ref = refs
        if first:
            big_ref[...] = jnp.full(big_ref.shape, NEG, jnp.float32)
            acc_ref[...] = jnp.zeros(acc_ref.shape, jnp.float32)
        else:
            big_ref[...] = big_in[...]
            acc_ref[...] = acc_in[...]
        blocks = [pl.ds(at, step) for at in range(0, rows, step)]
        for s, offset in enumerate(offsets):
            cache_ref = seg[s]
            size = cache_ref.shape[0] // 2
            count = jnp.max(live_ref[offset:offset + 1, :])

            @pl.when(count > 0)
            def _():
                live = lax.broadcasted_iota(jnp.int32, (size, width), 0) < count
                keys = jnp.where(live, cache_ref[:size, :], cache_ref[:1, :])
                turned = with_ones(cache_ref[size:, :])
                turned = jnp.where(
                    lax.broadcasted_iota(jnp.int32, turned.shape, 1) < count, turned, jnp.zeros_like(turned)
                )
                for at in blocks:
                    score = nt(keys, q_ref[at, :])
                    score_ref[:, at] = score
                    peak_ref[:, at] = jnp.max(score, axis=0, keepdims=True)
                for at in blocks:
                    big = big_ref[:, at]
                    new_big = jnp.maximum(big, peak_ref[:, at])
                    weight = jnp.exp2((score_ref[:, at] - new_big) * factor).astype(jnp.bfloat16)
                    fade = jnp.exp2((big - new_big) * factor)
                    acc_ref[:, at] = acc_ref[:, at] * fade + nn(turned, weight)
                    big_ref[:, at] = new_big

        if last:
            for i in range(rows // step):
                at = i * step
                total = acc_ref[width:width + 1, pl.ds(at, step)]
                done = (acc_ref[:width, pl.ds(at, step)] * (1.0 / total)).astype(jnp.bfloat16)
                outt_ref[:, pl.ds(at, step)] = done
                out_ref[pl.ds(at, step), :] = done.T

    arrays = [queries] + [a for _, a in segments] + ([] if first else list(state))
    scratch = [pltpu.VMEM(s, d) for s, d in shapes] if last else []
    scratch += [
        pltpu.VMEM((segments[0][1].shape[0] // 2, rows), jnp.float32), pltpu.VMEM((1, rows), jnp.float32)
    ]
    return call(
        kernel, ends if last else shapes, [], [live] + arrays, scratch,
        hbm_out=(0,) if last else (),
    )


def gradient_half(start, half, q_ref, prob_ref, cast_ref, diff_ref, inner_ref, values_ref, grad_ref, dscore_ref, scale):
    rows, width = q_ref.shape
    step = row_block(rows)
    values = values_ref[pl.ds(start, half), :]
    for at in range(0, rows, step):
        at = pl.ds(at, step)
        slope = nt(values, diff_ref[at, :]) - inner_ref[:, at]
        dscore_ref[:, at] = (prob_ref[pl.ds(start, half), at] * slope).astype(jnp.bfloat16)
    grad_ref[:, width:] = nn(cast_ref[pl.ds(start, half), :], diff_ref[...])
    grad_ref[:, :width] = nn(dscore_ref[...], q_ref[...]) * scale


def student(queries, teach, slots, other, per, half, scale):
    rounds = len(slots)
    rows, width = queries.shape
    step = row_block(rows)
    pieces = slots[0].shape[0] // per
    count = 2 * rounds * pieces * per
    factor = scale * math.log2(math.e)

    def kernel(q_ref, teach_ref, *refs):
        sources, refs = refs[: 2 * rounds], refs[2 * rounds:]
        grad_ref, prob_ref, cast_ref, diff_ref, inner_ref, values_ref, loss_ref, keys_ref, dscore_ref = refs
        n_chip, n_qry = lax.axis_size("keys") // 2, lax.axis_size("qry")
        me, mine = lax.axis_index("keys"), lax.axis_index("qry")
        core, chip = lax.rem(me, 2), lax.div(me, 2)
        for r, source in enumerate(sources):
            c, x = (core, r) if r < rounds else (1 - core, r - rounds)
            for d in range(pieces):
                place = (c * n_chip + (chip ^ x)) * n_qry + lax.rem(mine - d + n_qry, n_qry)
                to = pl.multiple_of(place * per, per)
                piece = source[pl.ds(d * per, per), :]
                keys_ref[pl.ds(to, per), :] = piece[:, :width]
                values_ref[pl.ds(to, per), :] = piece[:, width:]
        turned = with_ones(values_ref[...])
        squares = jnp.zeros((width, step), jnp.float32)
        blocks = [pl.ds(at, step) for at in range(0, rows, step)]
        for at in blocks:
            score = nt(keys_ref[...], q_ref[at, :])
            prob_ref[:, at] = score
            inner_ref[:, at] = jnp.max(score, axis=0, keepdims=True)
        for at in blocks:
            weight = jnp.exp2((prob_ref[:, at] - inner_ref[:, at]) * factor)
            prob_ref[:, at] = weight
            inner_ref[:, at] = 1.0 / jnp.sum(weight, axis=0, keepdims=True)
        for at in blocks:
            prob = prob_ref[:, at] * inner_ref[:, at]
            prob_ref[:, at] = prob
            cast = prob.astype(jnp.bfloat16)
            cast_ref[:, at] = cast
            both = nn(turned, cast)
            out, mass = both[:width, :], both[width:width + 1, :]
            diff = out - teach_ref[:, at].astype(jnp.float32)
            squares = squares + diff * diff
            short = diff.astype(jnp.bfloat16)
            diff_ref[at, :] = short.T
            inner_ref[:, at] = jnp.sum(short.astype(jnp.float32) * out, axis=0, keepdims=True) / mass
        loss_ref[...] = jnp.full(loss_ref.shape, jnp.sum(squares), jnp.float32)
        gradient_half(
            pl.multiple_of((1 - core) * half, half),
            half, q_ref, prob_ref, cast_ref, diff_ref, inner_ref, values_ref, grad_ref, dscore_ref, scale,
        )

    return call(
        kernel,
        [
            ((half, 2 * width), jnp.float32),
            ((count, rows), jnp.float32),
            ((count, rows), jnp.bfloat16),
            ((rows, width), jnp.bfloat16),
            ((1, rows), jnp.float32),
            ((count, width), jnp.bfloat16),
            ((PAD, LANES), jnp.float32),
        ],
        [], [queries, teach, *slots, *other],
        [pltpu.VMEM((count, width), jnp.bfloat16), pltpu.VMEM((half, rows), jnp.bfloat16)],
    )


def own_half(queries, prob, cast, diff, inner, values, half, scale):
    def kernel(*refs):
        start = pl.multiple_of(lax.rem(lax.axis_index("keys"), 2) * half, half)
        gradient_half(start, half, *refs, scale)

    return call(
        kernel, [((half, 2 * queries.shape[1]), jnp.float32)],
        [], [queries, prob, cast, diff, inner, values],
        [pltpu.VMEM((half, queries.shape[0]), jnp.bfloat16)],
    )[0]


def packed(own, got, loss, heard, per):
    half, wide = own.shape
    blocks = half // per

    def kernel(own_ref, got_ref, loss_ref, heard_ref, out_ref):
        squares = loss_ref[...] + heard_ref[...]
        one = squares.astype(jnp.bfloat16)
        left = squares - one.astype(jnp.float32)
        two = left.astype(jnp.bfloat16)
        three = (left - two.astype(jnp.float32)).astype(jnp.bfloat16)
        place = lax.broadcasted_iota(jnp.int32, (PAD, LANES), 0)
        zero = jnp.zeros((PAD, LANES), jnp.float32)
        parts = jnp.where(
            place == 0, one.astype(jnp.float32),
            jnp.where(place == 1, two.astype(jnp.float32), jnp.where(place == 2, three.astype(jnp.float32), zero)),
        ).astype(jnp.bfloat16)
        for b in range(blocks):
            at = b * per
            out_ref[b, :per, :] = (own_ref[pl.ds(at, per), :] + got_ref[pl.ds(at, per), :]).astype(jnp.bfloat16)
            for at in range(0, wide, LANES):
                out_ref[b, per:, pl.ds(at, LANES)] = parts

    return call(kernel, [((blocks, per + PAD, wide), jnp.bfloat16)], [], [own, got, loss, heard])[0]


def update(heard, slot_params, first_moment, second_moment, terms):
    per, wide = slot_params.shape

    def kernel(heard_ref, params_ref, first_ref, second_ref, grad_ref, p_ref, f_ref, s_ref, loss_ref):
        grad = jnp.zeros((per, wide), jnp.float32)
        tail = jnp.zeros((PAD, LANES), jnp.float32)
        for b in range(heard_ref.shape[0]):
            grad = grad + heard_ref[b, :per, :].astype(jnp.float32)
            tail = tail + heard_ref[b, per:, :LANES].astype(jnp.float32)
        grad_ref[...] = grad
        new_first = 0.9 * first_ref[...] + 0.1 * grad
        new_second = 0.95 * second_ref[...] + 0.05 * grad * grad
        f_ref[...] = new_first
        s_ref[...] = new_second
        p_ref[...] = params_ref[...] - 0.02 * new_first / (jnp.sqrt(new_second) + 1e-08)
        loss_ref[...] = jnp.sum(tail, axis=0, keepdims=True) / terms

    shape = ((per, wide), jnp.float32)
    return call(
        kernel, [shape] * 4 + [((1, LANES), jnp.float32)], [],
        [heard, slot_params, first_moment, second_moment], hbm_out=(0, 1, 2, 3, 4),
    )


def body(
    queries,
    cache_keys,
    cache_values,
    entry,
    visits,
    doc_length,
    slot_params,
    first_moment,
    second_moment,
):
    n_keys, n_qry = lax.axis_size("keys"), lax.axis_size("qry")
    tok, heads, width = queries.shape
    rows = tok * heads
    per = slot_params.shape[0]
    n_chip = n_keys // 2
    half = n_chip * n_qry * per
    scale = 1.0 / math.sqrt(width)

    def swap(block, bit):
        return lax.ppermute(block, "keys", [(k, k ^ bit) for k in range(n_keys)])

    copies, cache_own, flat = load(queries.reshape(rows, width), cache_keys, cache_values, slot_params)

    me, size = lax.axis_index("keys"), cache_keys.shape[0]
    shard = me ^ lax.broadcasted_iota(jnp.int32, (-(-n_keys // PAD) * PAD, LANES), 0)
    turn = lax.rem(shard - me - entry[0, 0] + 2 * n_keys, n_keys)
    live = jnp.where(turn < visits[0, 0], jnp.clip(doc_length[0] - shard * size, 0, size), 0)

    low = [0] + [j & -j for j in range(1, n_keys)]
    chips = range(2, n_keys, 2)

    cache = {0: cache_own}
    for j in list(chips) + list(range(1, n_keys, 2)):
        cache[j] = swap(cache[j ^ low[j]], low[j])

    column = [copies]
    for d in range(1, n_qry):
        column.append(lax.ppermute(copies, "qry", [(i, (i + d) % n_qry) for i in range(n_qry)]))
    slots = {0: jnp.concatenate(column, axis=0)}
    for j in chips:
        slots[j] = swap(slots[j ^ low[j]], low[j])
    other = [swap(slots[j], 1) for j in range(0, n_keys, 2)]
    slots = [slots[j] for j in range(0, n_keys, 2)]

    stages = [("own", [0]), ("partner", [1]), ("chip", list(chips)), ("far", list(range(3, n_keys, 2)))]
    stages = [stage for stage in stages if stage[1]]
    state = None
    for name, offsets in stages:
        last = name == stages[-1][0]
        state = teacher(live, flat, [(j, cache[j]) for j in offsets], state, last, scale)
    teacher_rows, teacher_turned = state

    away, prob, cast, diff, inner, values, loss = student(flat, teacher_turned, slots, other, per, half, scale)
    own = own_half(flat, prob, cast, diff, inner, values, half, scale)
    sent = packed(own, swap(away, 1), loss, swap(loss, 1), per)

    groups = [[(2 * x + c) * n_qry + q for x in range(n_chip) for q in range(n_qry)] for c in range(2)]
    heard = lax.all_to_all(sent, ("keys", "qry"), 0, 0, axis_index_groups=groups, tiled=True)
    slot_grad, new_params, new_first, new_second, loss = update(
        heard, slot_params, first_moment, second_moment, rows * n_keys * n_qry
    )
    teacher_out = teacher_rows.reshape(tok, heads, width)
    return (teacher_out, slot_grad, new_params, new_first, new_second, loss[0, :1])


def solution(mesh):
    return jax.shard_map(
        body,
        mesh=mesh,
        in_specs=(
            P(("grp", "keys", "qry"), None, None),
            P(("grp", "keys"), None),
            P(("grp", "keys"), None),
            P(("grp", "keys"), "qry"),
            P(("grp", "keys"), "qry"),
            P("grp"),
            P(("grp", "keys", "qry"), None),
            P(("grp", "keys", "qry"), None),
            P(("grp", "keys", "qry"), None),
        ),
        out_specs=(
            P(("grp", "keys", "qry"), None, None),
            P(("grp", "keys", "qry"), None),
            P(("grp", "keys", "qry"), None),
            P(("grp", "keys", "qry"), None),
            P(("grp", "keys", "qry"), None),
            P("grp"),
        ),
        check_vma=False,
    )
```

```python
import math

import jax
import jax.numpy as jnp
from jax import lax
from jax.experimental import pallas as pl
from jax.experimental.pallas import tpu as pltpu
from jax.sharding import PartitionSpec as P


NEG = -1e30
PAD = 8
LANES = 128
TILE = 128
GRANT = 24 * 2**20


def nt(left, right):
    return lax.dot_general(left, right, (((1,), (1,)), ((), ())), preferred_element_type=jnp.float32)


def nn(left, right):
    return jnp.dot(left, right, preferred_element_type=jnp.float32)


def with_ones(values):
    turned = values.T
    return jnp.concatenate([turned, jnp.ones((PAD, turned.shape[1]), turned.dtype)], axis=0)


def fold(block, join):
    groups = [block[r:r + PAD] for r in range(0, block.shape[0], PAD)]
    while len(groups) > 1:
        groups = [join(*groups[g:g + 2]) if g + 1 < len(groups) else groups[g] for g in range(0, len(groups), 2)]
    return groups[0]


def row_block(rows):
    return math.gcd(rows, 256)


def call(kernel, out, arrays, scratch=(), hbm_out=()):
    vm, hbm = pl.BlockSpec(memory_space=pltpu.VMEM), pl.BlockSpec(memory_space=pltpu.HBM)
    arrays = [pltpu.with_memory_space_constraint(a, pltpu.VMEM) for a in arrays]
    spaces = [pltpu.HBM if i in hbm_out else pltpu.VMEM for i in range(len(out))]
    return pl.pallas_call(
        kernel,
        out_shape=tuple(space(s, d) for space, (s, d) in zip(spaces, out)),
        in_specs=[vm] * len(arrays),
        out_specs=tuple(hbm if i in hbm_out else vm for i in range(len(out))),
        scratch_shapes=list(scratch),
        compiler_params=pltpu.CompilerParams(vmem_limit_bytes=GRANT),
    )(*arrays)


def load(queries, keys, values, slot_params):
    size, width = keys.shape
    ins = [pltpu.with_memory_space_constraint(a, pltpu.HBM) for a in (slot_params, keys, values, queries)]

    def kernel(*refs):
        sources, (slots_ref, cache_ref, q_ref, full_ref, sems) = refs[:4], refs[4:]
        targets = (full_ref, cache_ref.at[pl.ds(0, size)], cache_ref.at[pl.ds(size, size)], q_ref)
        moves = [pltpu.make_async_copy(a, b, sems.at[i]) for i, (a, b) in enumerate(zip(sources, targets))]
        for move in moves:
            move.start()
        moves[0].wait()
        slots_ref[...] = full_ref[...].astype(jnp.bfloat16)
        for move in moves[1:]:
            move.wait()

    return pl.pallas_call(
        kernel,
        out_shape=(
            pltpu.VMEM(slot_params.shape, jnp.bfloat16),
            pltpu.VMEM((2 * size, width), keys.dtype),
            pltpu.VMEM(queries.shape, queries.dtype),
        ),
        in_specs=[pl.BlockSpec(memory_space=pltpu.HBM)] * 4,
        out_specs=(pl.BlockSpec(memory_space=pltpu.VMEM),) * 3,
        scratch_shapes=[
            pltpu.VMEM(slot_params.shape, slot_params.dtype),
            pltpu.SemaphoreType.DMA((4,)),
        ],
        compiler_params=pltpu.CompilerParams(vmem_limit_bytes=GRANT),
        name="load",
    )(*ins)


def teacher(live, queries, segments, state, last, scale):
    rows, width = queries.shape
    step = row_block(rows)
    shapes = [((1, rows), jnp.float32), ((width + PAD, rows), jnp.float32)]
    ends = [((rows, width), jnp.bfloat16), ((width, rows), jnp.bfloat16)]
    offsets = [j for j, _ in segments]
    first = state is None
    factor = scale * math.log2(math.e)

    def kernel(live_ref, q_ref, *refs):
        seg, refs = refs[: len(offsets)], refs[len(offsets):]
        if not first:
            (big_in, acc_in), refs = refs[:2], refs[2:]
        if last:
            (out_ref, outt_ref), refs = refs[:2], refs[2:]
        big_ref, acc_ref, score_ref, peak_ref = refs
        if first:
            big_ref[...] = jnp.full(big_ref.shape, NEG, jnp.float32)
            acc_ref[...] = jnp.zeros(acc_ref.shape, jnp.float32)
        else:
            big_ref[...] = big_in[...]
            acc_ref[...] = acc_in[...]
        blocks = [pl.ds(at, step) for at in range(0, rows, step)]
        for s, offset in enumerate(offsets):
            cache_ref = seg[s]
            size = cache_ref.shape[0] // 2
            count = jnp.max(live_ref[offset:offset + 1, :])

            @pl.when(count > 0)
            def _():
                live = lax.broadcasted_iota(jnp.int32, (size, width), 0) < count
                keys = jnp.where(live, cache_ref[:size, :], cache_ref[:1, :])
                turned = with_ones(cache_ref[size:, :])
                turned = jnp.where(
                    lax.broadcasted_iota(jnp.int32, turned.shape, 1) < count, turned, jnp.zeros_like(turned)
                )
                for at in blocks:
                    peak = jnp.full((PAD, step), NEG, jnp.float32)
                    for t in range(0, size, TILE):
                        score = nt(keys[t:t + TILE], q_ref[at, :])
                        score_ref[t:t + TILE, at] = score
                        peak = jnp.maximum(peak, fold(score, jnp.maximum))
                    peak_ref[:, at] = jnp.max(peak, axis=0, keepdims=True)
                for at in blocks:
                    big = big_ref[:, at]
                    new_big = jnp.maximum(big, peak_ref[:, at])
                    weight = jnp.exp2((score_ref[:, at] - new_big) * factor).astype(jnp.bfloat16)
                    fade = jnp.exp2((big - new_big) * factor)
                    acc_ref[:, at] = acc_ref[:, at] * fade + nn(turned, weight)
                    big_ref[:, at] = new_big

        if last:
            for i in range(rows // step):
                at = i * step
                total = acc_ref[width:width + 1, pl.ds(at, step)]
                done = (acc_ref[:width, pl.ds(at, step)] * (1.0 / total)).astype(jnp.bfloat16)
                outt_ref[:, pl.ds(at, step)] = done
                out_ref[pl.ds(at, step), :] = done.T

    arrays = [queries] + [a for _, a in segments] + ([] if first else list(state))
    scratch = [pltpu.VMEM(s, d) for s, d in shapes] if last else []
    scratch += [
        pltpu.VMEM((segments[0][1].shape[0] // 2, rows), jnp.float32), pltpu.VMEM((1, rows), jnp.float32)
    ]
    return call(kernel, ends if last else shapes, [live] + arrays, scratch)


def gradient_half(start, half, q_ref, prob_ref, cast_ref, diff_ref, inner_ref, values_ref, grad_ref, dscore_ref, scale):
    rows, width = q_ref.shape
    step = row_block(rows)
    values = values_ref[pl.ds(start, half), :]
    for at in range(0, rows, step):
        at = pl.ds(at, step)
        slope = nt(values, diff_ref[at, :]) - inner_ref[:, at]
        dscore_ref[:, at] = (prob_ref[pl.ds(start, half), at] * slope).astype(jnp.bfloat16)
    grad_ref[:, width:] = nn(cast_ref[pl.ds(start, half), :], diff_ref[...])
    grad_ref[:, :width] = nn(dscore_ref[...], q_ref[...]) * scale


def student(queries, teach, slots, other, per, half, scale):
    rounds = len(slots)
    rows, width = queries.shape
    step = row_block(rows)
    pieces = slots[0].shape[0] // per
    count = 2 * rounds * pieces * per
    factor = scale * math.log2(math.e)

    def kernel(q_ref, teach_ref, *refs):
        sources, refs = refs[: 2 * rounds], refs[2 * rounds:]
        grad_ref, prob_ref, cast_ref, diff_ref, inner_ref, values_ref, loss_ref, keys_ref, dscore_ref = refs
        n_chip, n_qry = lax.axis_size("keys") // 2, lax.axis_size("qry")
        me, mine = lax.axis_index("keys"), lax.axis_index("qry")
        core, chip = lax.rem(me, 2), lax.div(me, 2)
        for r, source in enumerate(sources):
            c, x = (core, r) if r < rounds else (1 - core, r - rounds)
            for d in range(pieces):
                place = (c * n_chip + (chip ^ x)) * n_qry + lax.rem(mine - d + n_qry, n_qry)
                to = pl.multiple_of(place * per, per)
                piece = source[pl.ds(d * per, per), :]
                keys_ref[pl.ds(to, per), :] = piece[:, :width]
                values_ref[pl.ds(to, per), :] = piece[:, width:]
        turned = with_ones(values_ref[...])
        squares = jnp.zeros((width, step), jnp.float32)
        blocks = [pl.ds(at, step) for at in range(0, rows, step)]
        for at in blocks:
            score = nt(keys_ref[...], q_ref[at, :])
            prob_ref[:, at] = score
            inner_ref[:, at] = jnp.max(score, axis=0, keepdims=True)
        for at in blocks:
            weight = jnp.exp2((prob_ref[:, at] - inner_ref[:, at]) * factor)
            prob_ref[:, at] = weight
            inner_ref[:, at] = 1.0 / jnp.sum(weight, axis=0, keepdims=True)
        for at in blocks:
            prob = prob_ref[:, at] * inner_ref[:, at]
            prob_ref[:, at] = prob
            cast = prob.astype(jnp.bfloat16)
            cast_ref[:, at] = cast
            both = nn(turned, cast)
            out, mass = both[:width, :], both[width:width + 1, :]
            diff = out - teach_ref[:, at].astype(jnp.float32)
            squares = squares + diff * diff
            short = diff.astype(jnp.bfloat16)
            diff_ref[at, :] = short.T
            inner_ref[:, at] = jnp.sum(short.astype(jnp.float32) * out, axis=0, keepdims=True) / mass
        loss_ref[...] = jnp.full(loss_ref.shape, jnp.sum(squares), jnp.float32)
        gradient_half(
            pl.multiple_of((1 - core) * half, half),
            half, q_ref, prob_ref, cast_ref, diff_ref, inner_ref, values_ref, grad_ref, dscore_ref, scale,
        )

    return call(
        kernel,
        [
            ((half, 2 * width), jnp.float32),
            ((count, rows), jnp.float32),
            ((count, rows), jnp.bfloat16),
            ((rows, width), jnp.bfloat16),
            ((1, rows), jnp.float32),
            ((count, width), jnp.bfloat16),
            ((PAD, LANES), jnp.float32),
        ],
        [queries, teach, *slots, *other],
        [pltpu.VMEM((count, width), jnp.bfloat16), pltpu.VMEM((half, rows), jnp.bfloat16)],
    )


def own_half(queries, teach_rows, prob, cast, diff, inner, values, half, scale):
    rows, width = queries.shape

    def kernel(rows_ref, q_ref, prob_ref, cast_ref, diff_ref, inner_ref, values_ref, *refs):
        grad_ref, out_ref, dscore_ref, sem = refs
        write = pltpu.make_async_copy(rows_ref, out_ref, sem)
        write.start()
        start = pl.multiple_of(lax.rem(lax.axis_index("keys"), 2) * half, half)
        gradient_half(
            start, half, q_ref, prob_ref, cast_ref, diff_ref, inner_ref, values_ref, grad_ref, dscore_ref, scale
        )
        write.wait()

    return call(
        kernel, [((half, 2 * width), jnp.float32), ((rows, width), jnp.bfloat16)],
        [teach_rows, queries, prob, cast, diff, inner, values],
        [pltpu.VMEM((half, rows), jnp.bfloat16), pltpu.SemaphoreType.DMA(())], hbm_out=(1,),
    )


def packed(own, got, loss, heard, per):
    half, wide = own.shape
    blocks = half // per

    def kernel(own_ref, got_ref, loss_ref, heard_ref, out_ref):
        squares = loss_ref[...] + heard_ref[...]
        one = squares.astype(jnp.bfloat16)
        left = squares - one.astype(jnp.float32)
        two = left.astype(jnp.bfloat16)
        three = (left - two.astype(jnp.float32)).astype(jnp.bfloat16)
        place = lax.broadcasted_iota(jnp.int32, (PAD, LANES), 0)
        zero = jnp.zeros((PAD, LANES), jnp.float32)
        parts = jnp.where(
            place == 0, one.astype(jnp.float32),
            jnp.where(place == 1, two.astype(jnp.float32), jnp.where(place == 2, three.astype(jnp.float32), zero)),
        ).astype(jnp.bfloat16)
        for b in range(blocks):
            at = b * per
            out_ref[b, :per, :] = (own_ref[pl.ds(at, per), :] + got_ref[pl.ds(at, per), :]).astype(jnp.bfloat16)
            for at in range(0, wide, LANES):
                out_ref[b, per:, pl.ds(at, LANES)] = parts

    return call(kernel, [((blocks, per + PAD, wide), jnp.bfloat16)], [own, got, loss, heard])[0]


def update(heard, slot_params, first_moment, second_moment, terms):
    per, wide = slot_params.shape

    def kernel(heard_ref, params_ref, first_ref, second_ref, *refs):
        outs, bufs, sems = refs[:5], refs[5:10], refs[10]
        moves = [pltpu.make_async_copy(b, o, sems.at[i]) for i, (b, o) in enumerate(zip(bufs, outs))]
        grad = jnp.zeros((per, wide), jnp.float32)
        tail = jnp.zeros((PAD, LANES), jnp.float32)
        for b in range(heard_ref.shape[0]):
            grad = grad + heard_ref[b, :per, :].astype(jnp.float32)
            tail = tail + heard_ref[b, per:, :LANES].astype(jnp.float32)
        bufs[0][...] = grad
        moves[0].start()
        new_first = 0.9 * first_ref[...] + 0.1 * grad
        bufs[2][...] = new_first
        moves[2].start()
        new_second = 0.95 * second_ref[...] + 0.05 * grad * grad
        bufs[3][...] = new_second
        moves[3].start()
        bufs[4][...] = jnp.sum(tail, axis=0, keepdims=True) / terms
        moves[4].start()
        bufs[1][...] = params_ref[...] - 0.02 * new_first / (jnp.sqrt(new_second) + 1e-08)
        moves[1].start()
        for move in moves:
            move.wait()

    outs = [((per, wide), jnp.float32)] * 4 + [((1, LANES), jnp.float32)]
    return call(
        kernel, outs, [heard, slot_params, first_moment, second_moment],
        [pltpu.VMEM(s, d) for s, d in outs] + [pltpu.SemaphoreType.DMA((5,))], hbm_out=(0, 1, 2, 3, 4),
    )


def body(
    queries,
    cache_keys,
    cache_values,
    entry,
    visits,
    doc_length,
    slot_params,
    first_moment,
    second_moment,
):
    n_keys, n_qry = lax.axis_size("keys"), lax.axis_size("qry")
    tok, heads, width = queries.shape
    rows = tok * heads
    per = slot_params.shape[0]
    n_chip = n_keys // 2
    half = n_chip * n_qry * per
    scale = 1.0 / math.sqrt(width)

    def swap(block, bit):
        return lax.ppermute(block, "keys", [(k, k ^ bit) for k in range(n_keys)])

    copies, cache_own, flat = load(queries.reshape(rows, width), cache_keys, cache_values, slot_params)

    me, size = lax.axis_index("keys"), cache_keys.shape[0]
    shard = me ^ lax.broadcasted_iota(jnp.int32, (-(-n_keys // PAD) * PAD, LANES), 0)
    turn = lax.rem(shard - me - entry[0, 0] + 2 * n_keys, n_keys)
    live = jnp.where(turn < visits[0, 0], jnp.clip(doc_length[0] - shard * size, 0, size), 0)

    low = [0] + [j & -j for j in range(1, n_keys)]
    chips = range(2, n_keys, 2)

    cache = {0: cache_own}
    for j in list(chips) + list(range(1, n_keys, 2)):
        cache[j] = swap(cache[j ^ low[j]], low[j])

    column = [copies]
    for d in range(1, n_qry):
        column.append(lax.ppermute(copies, "qry", [(i, (i + d) % n_qry) for i in range(n_qry)]))
    slots = {0: jnp.concatenate(column, axis=0)}
    for j in chips:
        slots[j] = swap(slots[j ^ low[j]], low[j])
    other = [swap(slots[j], 1) for j in range(0, n_keys, 2)]
    slots = [slots[j] for j in range(0, n_keys, 2)]

    stages = [("own", [0]), ("partner", [1]), ("chip", list(chips)), ("far", list(range(3, n_keys, 2)))]
    stages = [stage for stage in stages if stage[1]]
    state = None
    for name, offsets in stages:
        last = name == stages[-1][0]
        state = teacher(live, flat, [(j, cache[j]) for j in offsets], state, last, scale)
    teacher_rows, teacher_turned = state

    away, prob, cast, diff, inner, values, loss = student(flat, teacher_turned, slots, other, per, half, scale)
    own, teacher_out = own_half(flat, teacher_rows, prob, cast, diff, inner, values, half, scale)
    sent = packed(own, swap(away, 1), loss, swap(loss, 1), per)

    groups = [[(2 * x + c) * n_qry + q for x in range(n_chip) for q in range(n_qry)] for c in range(2)]
    heard = lax.all_to_all(sent, ("keys", "qry"), 0, 0, axis_index_groups=groups, tiled=True)
    slot_grad, new_params, new_first, new_second, loss = update(
        heard, slot_params, first_moment, second_moment, rows * n_keys * n_qry
    )
    teacher_out = teacher_out.reshape(tok, heads, width)
    return (teacher_out, slot_grad, new_params, new_first, new_second, loss[0, :1])


def solution(mesh):
    return jax.shard_map(
        body,
        mesh=mesh,
        in_specs=(
            P(("grp", "keys", "qry"), None, None),
            P(("grp", "keys"), None),
            P(("grp", "keys"), None),
            P(("grp", "keys"), "qry"),
            P(("grp", "keys"), "qry"),
            P("grp"),
            P(("grp", "keys", "qry"), None),
            P(("grp", "keys", "qry"), None),
            P(("grp", "keys", "qry"), None),
        ),
        out_specs=(
            P(("grp", "keys", "qry"), None, None),
            P(("grp", "keys", "qry"), None),
            P(("grp", "keys", "qry"), None),
            P(("grp", "keys", "qry"), None),
            P(("grp", "keys", "qry"), None),
            P("grp"),
        ),
        check_vma=False,
    )
```

```python
import math

import jax
import jax.numpy as jnp
from jax import lax
from jax.experimental import pallas as pl
from jax.experimental.pallas import tpu as pltpu
from jax.sharding import PartitionSpec as P


NEG = -1e30
PAD = 8
LANES = 128
TILE = 128
GRANT = 24 * 2**20


def nt(left, right):
    return lax.dot_general(left, right, (((1,), (1,)), ((), ())), preferred_element_type=jnp.float32)


def nn(left, right):
    return jnp.dot(left, right, preferred_element_type=jnp.float32)


def with_ones(values):
    turned = values.T
    return jnp.concatenate([turned, jnp.ones((PAD, turned.shape[1]), turned.dtype)], axis=0)


def fold(block, join):
    groups = [block[r:r + PAD] for r in range(0, block.shape[0], PAD)]
    while len(groups) > 1:
        groups = [join(*groups[g:g + 2]) if g + 1 < len(groups) else groups[g] for g in range(0, len(groups), 2)]
    return groups[0]


def peer(index, d, count):
    if count & (count - 1):
        return (index - d + count) % count if isinstance(index, int) else lax.rem(index - d + count, count)
    return index ^ d


def row_block(rows):
    return math.gcd(rows, 256)


def call(kernel, out, arrays, scratch=(), hbm_out=()):
    vm, hbm = pl.BlockSpec(memory_space=pltpu.VMEM), pl.BlockSpec(memory_space=pltpu.HBM)
    arrays = [pltpu.with_memory_space_constraint(a, pltpu.VMEM) for a in arrays]
    spaces = [pltpu.HBM if i in hbm_out else pltpu.VMEM for i in range(len(out))]
    return pl.pallas_call(
        kernel,
        out_shape=tuple(space(s, d) for space, (s, d) in zip(spaces, out)),
        in_specs=[vm] * len(arrays),
        out_specs=tuple(hbm if i in hbm_out else vm for i in range(len(out))),
        scratch_shapes=list(scratch),
        compiler_params=pltpu.CompilerParams(vmem_limit_bytes=GRANT),
    )(*arrays)


def load(queries, keys, values, slot_params):
    size, width = keys.shape
    ins = [pltpu.with_memory_space_constraint(a, pltpu.HBM) for a in (slot_params, keys, values, queries)]

    def kernel(*refs):
        sources, (slots_ref, cache_ref, q_ref, full_ref, sems) = refs[:4], refs[4:]
        targets = (full_ref, cache_ref.at[pl.ds(0, size)], cache_ref.at[pl.ds(size, size)], q_ref)
        moves = [pltpu.make_async_copy(a, b, sems.at[i]) for i, (a, b) in enumerate(zip(sources, targets))]
        for move in moves:
            move.start()
        moves[0].wait()
        slots_ref[...] = full_ref[...].astype(jnp.bfloat16)
        for move in moves[1:]:
            move.wait()

    return pl.pallas_call(
        kernel,
        out_shape=(
            pltpu.VMEM(slot_params.shape, jnp.bfloat16),
            pltpu.VMEM((2 * size, width), keys.dtype),
            pltpu.VMEM(queries.shape, queries.dtype),
        ),
        in_specs=[pl.BlockSpec(memory_space=pltpu.HBM)] * 4,
        out_specs=(pl.BlockSpec(memory_space=pltpu.VMEM),) * 3,
        scratch_shapes=[
            pltpu.VMEM(slot_params.shape, slot_params.dtype),
            pltpu.SemaphoreType.DMA((4,)),
        ],
        compiler_params=pltpu.CompilerParams(vmem_limit_bytes=GRANT),
        name="load",
    )(*ins)


def teacher(live, queries, segments, state, last, scale):
    rows, width = queries.shape
    step = row_block(rows)
    shapes = [((1, rows), jnp.float32), ((width + PAD, rows), jnp.float32)]
    ends = [((rows, width), jnp.bfloat16), ((width, rows), jnp.bfloat16)]
    offsets = [j for j, _ in segments]
    first = state is None
    factor = scale * math.log2(math.e)

    def kernel(live_ref, q_ref, *refs):
        seg, refs = refs[: len(offsets)], refs[len(offsets):]
        if not first:
            (big_in, acc_in), refs = refs[:2], refs[2:]
        if last:
            (out_ref, outt_ref), refs = refs[:2], refs[2:]
        big_ref, acc_ref, score_ref, peak_ref = refs
        if first:
            big_ref[...] = jnp.full(big_ref.shape, NEG, jnp.float32)
            acc_ref[...] = jnp.zeros(acc_ref.shape, jnp.float32)
        else:
            big_ref[...] = big_in[...]
            acc_ref[...] = acc_in[...]
        blocks = [pl.ds(at, step) for at in range(0, rows, step)]
        for s, offset in enumerate(offsets):
            cache_ref = seg[s]
            size = cache_ref.shape[0] // 2
            tile = math.gcd(size, TILE)
            count = jnp.max(live_ref[offset:offset + 1, :])

            @pl.when(count > 0)
            def _():
                live = lax.broadcasted_iota(jnp.int32, (size, width), 0) < count
                keys = jnp.where(live, cache_ref[:size, :], cache_ref[:1, :])
                turned = with_ones(cache_ref[size:, :])
                turned = jnp.where(
                    lax.broadcasted_iota(jnp.int32, turned.shape, 1) < count, turned, jnp.zeros_like(turned)
                )
                for at in blocks:
                    peak = jnp.full((PAD, step), NEG, jnp.float32)
                    for t in range(0, size, tile):
                        score = nt(keys[t:t + tile], q_ref[at, :])
                        score_ref[t:t + tile, at] = score
                        peak = jnp.maximum(peak, fold(score, jnp.maximum))
                    peak_ref[:, at] = jnp.max(peak, axis=0, keepdims=True)
                for at in blocks:
                    big = big_ref[:, at]
                    new_big = jnp.maximum(big, peak_ref[:, at])
                    weight = jnp.exp2((score_ref[:, at] - new_big) * factor).astype(jnp.bfloat16)
                    fade = jnp.exp2((big - new_big) * factor)
                    acc_ref[:, at] = acc_ref[:, at] * fade + nn(turned, weight)
                    big_ref[:, at] = new_big

        if last:
            for i in range(rows // step):
                at = i * step
                total = acc_ref[width:width + 1, pl.ds(at, step)]
                done = (acc_ref[:width, pl.ds(at, step)] * (1.0 / total)).astype(jnp.bfloat16)
                outt_ref[:, pl.ds(at, step)] = done
                out_ref[pl.ds(at, step), :] = done.T

    arrays = [queries] + [a for _, a in segments] + ([] if first else list(state))
    scratch = [pltpu.VMEM(s, d) for s, d in shapes] if last else []
    scratch += [
        pltpu.VMEM((segments[0][1].shape[0] // 2, rows), jnp.float32), pltpu.VMEM((1, rows), jnp.float32)
    ]
    return call(kernel, ends if last else shapes, [live] + arrays, scratch)


def gradient_half(start, half, q_ref, prob_ref, cast_ref, diff_ref, inner_ref, values_ref, grad_ref, dscore_ref, scale):
    rows, width = q_ref.shape
    step = row_block(rows)
    values = values_ref[pl.ds(start, half), :]
    for at in range(0, rows, step):
        at = pl.ds(at, step)
        slope = nt(values, diff_ref[at, :]) - inner_ref[:, at]
        dscore_ref[:, at] = (prob_ref[pl.ds(start, half), at] * slope).astype(jnp.bfloat16)
    grad_ref[:half, width:] = nn(cast_ref[pl.ds(start, half), :], diff_ref[...])
    grad_ref[:half, :width] = nn(dscore_ref[...], q_ref[...]) * scale


def student(queries, teach, slots, other, per, half, scale):
    rounds = len(slots)
    rows, width = queries.shape
    step = row_block(rows)
    pieces = slots[0].shape[0] // per
    count = 2 * rounds * pieces * per
    tile = math.gcd(count, TILE)
    factor = scale * math.log2(math.e)

    def kernel(q_ref, teach_ref, *refs):
        sources, refs = refs[: 2 * rounds], refs[2 * rounds:]
        grad_ref, prob_ref, cast_ref, diff_ref, inner_ref, values_ref, keys_ref, dscore_ref = refs
        n_chip, n_qry = lax.axis_size("keys") // 2, lax.axis_size("qry")
        me, mine = lax.axis_index("keys"), lax.axis_index("qry")
        core, chip = lax.rem(me, 2), lax.div(me, 2)
        for r, source in enumerate(sources):
            c, x = (core, r) if r < rounds else (1 - core, r - rounds)
            for d in range(pieces):
                place = (c * n_chip + (chip ^ x)) * n_qry + peer(mine, d, n_qry)
                to = pl.multiple_of(place * per, per)
                piece = source[pl.ds(d * per, per), :]
                keys_ref[pl.ds(to, per), :] = piece[:, :width]
                values_ref[pl.ds(to, per), :] = piece[:, width:]
        turned = with_ones(values_ref[...])
        squares = jnp.zeros((width, step), jnp.float32)
        blocks = [pl.ds(at, step) for at in range(0, rows, step)]
        for at in blocks:
            peak = jnp.full((PAD, step), NEG, jnp.float32)
            for t in range(0, count, tile):
                score = nt(keys_ref[t:t + tile, :], q_ref[at, :])
                prob_ref[t:t + tile, at] = score
                peak = jnp.maximum(peak, fold(score, jnp.maximum))
            inner_ref[:, at] = jnp.max(peak, axis=0, keepdims=True)
        for at in blocks:
            total = jnp.zeros((PAD, step), jnp.float32)
            for t in range(0, count, tile):
                weight = jnp.exp2((prob_ref[t:t + tile, at] - inner_ref[:, at]) * factor)
                prob_ref[t:t + tile, at] = weight
                total = total + fold(weight, jnp.add)
            inner_ref[:, at] = 1.0 / jnp.sum(total, axis=0, keepdims=True)
        for at in blocks:
            prob = prob_ref[:, at] * inner_ref[:, at]
            prob_ref[:, at] = prob
            cast = prob.astype(jnp.bfloat16)
            cast_ref[:, at] = cast
            both = nn(turned, cast)
            out, mass = both[:width, :], both[width:width + 1, :]
            diff = out - teach_ref[:, at].astype(jnp.float32)
            squares = squares + diff * diff
            short = diff.astype(jnp.bfloat16)
            diff_ref[at, :] = short.T
            inner_ref[:, at] = jnp.sum(short.astype(jnp.float32) * out, axis=0, keepdims=True) / mass
        grad_ref[half:, :] = jnp.full((PAD, 2 * width), jnp.sum(squares), jnp.float32)
        gradient_half(
            pl.multiple_of((1 - core) * half, half),
            half, q_ref, prob_ref, cast_ref, diff_ref, inner_ref, values_ref, grad_ref, dscore_ref, scale,
        )

    return call(
        kernel,
        [
            ((half + PAD, 2 * width), jnp.float32),
            ((count, rows), jnp.float32),
            ((count, rows), jnp.bfloat16),
            ((rows, width), jnp.bfloat16),
            ((1, rows), jnp.float32),
            ((count, width), jnp.bfloat16),
        ],
        [queries, teach, *slots, *other],
        [pltpu.VMEM((count, width), jnp.bfloat16), pltpu.VMEM((half, rows), jnp.bfloat16)],
    )


def own_half(queries, teach_rows, prob, cast, diff, inner, values, half, scale):
    rows, width = queries.shape

    def kernel(rows_ref, q_ref, prob_ref, cast_ref, diff_ref, inner_ref, values_ref, *refs):
        grad_ref, out_ref, dscore_ref, sem = refs
        write = pltpu.make_async_copy(rows_ref, out_ref, sem)
        write.start()
        start = pl.multiple_of(lax.rem(lax.axis_index("keys"), 2) * half, half)
        gradient_half(
            start, half, q_ref, prob_ref, cast_ref, diff_ref, inner_ref, values_ref, grad_ref, dscore_ref, scale
        )
        write.wait()

    return call(
        kernel, [((half, 2 * width), jnp.float32), ((rows, width), jnp.bfloat16)],
        [teach_rows, queries, prob, cast, diff, inner, values],
        [pltpu.VMEM((half, rows), jnp.bfloat16), pltpu.SemaphoreType.DMA(())], hbm_out=(1,),
    )


def packed(own, away, got, per):
    half, wide = own.shape
    blocks = half // per

    def kernel(own_ref, away_ref, got_ref, out_ref):
        squares = away_ref[half:, :LANES] + got_ref[half:, :LANES]
        one = squares.astype(jnp.bfloat16)
        left = squares - one.astype(jnp.float32)
        two = left.astype(jnp.bfloat16)
        three = (left - two.astype(jnp.float32)).astype(jnp.bfloat16)
        place = lax.broadcasted_iota(jnp.int32, (PAD, LANES), 0)
        zero = jnp.zeros((PAD, LANES), jnp.float32)
        parts = jnp.where(
            place == 0, one.astype(jnp.float32),
            jnp.where(place == 1, two.astype(jnp.float32), jnp.where(place == 2, three.astype(jnp.float32), zero)),
        ).astype(jnp.bfloat16)
        for b in range(blocks):
            at = b * per
            out_ref[b, :per, :] = (own_ref[pl.ds(at, per), :] + got_ref[pl.ds(at, per), :]).astype(jnp.bfloat16)
            for at in range(0, wide, LANES):
                out_ref[b, per:, pl.ds(at, LANES)] = parts

    return call(kernel, [((blocks, per + PAD, wide), jnp.bfloat16)], [own, away, got])[0]


def update(heard, slot_params, first_moment, second_moment, terms):
    per, wide = slot_params.shape

    def kernel(heard_ref, params_ref, first_ref, second_ref, *refs):
        outs, bufs, sems = refs[:5], refs[5:10], refs[10]
        moves = [pltpu.make_async_copy(b, o, sems.at[i]) for i, (b, o) in enumerate(zip(bufs, outs))]
        grad = jnp.zeros((per, wide), jnp.float32)
        tail = jnp.zeros((PAD, LANES), jnp.float32)
        for b in range(heard_ref.shape[0]):
            grad = grad + heard_ref[b, :per, :].astype(jnp.float32)
            tail = tail + heard_ref[b, per:, :LANES].astype(jnp.float32)
        bufs[0][...] = grad
        moves[0].start()
        new_first = 0.9 * first_ref[...] + 0.1 * grad
        bufs[2][...] = new_first
        moves[2].start()
        new_second = 0.95 * second_ref[...] + 0.05 * grad * grad
        bufs[3][...] = new_second
        moves[3].start()
        bufs[4][...] = jnp.sum(tail, axis=0, keepdims=True) / terms
        moves[4].start()
        bufs[1][...] = params_ref[...] - 0.02 * new_first / (jnp.sqrt(new_second) + 1e-08)
        moves[1].start()
        for move in moves:
            move.wait()

    outs = [((per, wide), jnp.float32)] * 4 + [((1, LANES), jnp.float32)]
    return call(
        kernel, outs, [heard, slot_params, first_moment, second_moment],
        [pltpu.VMEM(s, d) for s, d in outs] + [pltpu.SemaphoreType.DMA((5,))], hbm_out=(0, 1, 2, 3, 4),
    )


def body(
    queries,
    cache_keys,
    cache_values,
    entry,
    visits,
    doc_length,
    slot_params,
    first_moment,
    second_moment,
):
    n_keys, n_qry = lax.axis_size("keys"), lax.axis_size("qry")
    tok, heads, width = queries.shape
    rows = tok * heads
    per = slot_params.shape[0]
    n_chip = n_keys // 2
    half = n_chip * n_qry * per
    scale = 1.0 / math.sqrt(width)

    def swap(block, bit):
        return lax.ppermute(block, "keys", [(k, k ^ bit) for k in range(n_keys)])

    copies, cache_own, flat = load(queries.reshape(rows, width), cache_keys, cache_values, slot_params)

    me, size = lax.axis_index("keys"), cache_keys.shape[0]
    shard = me ^ lax.broadcasted_iota(jnp.int32, (-(-n_keys // PAD) * PAD, LANES), 0)
    turn = lax.rem(shard - me - entry[0, 0] + 2 * n_keys, n_keys)
    live = jnp.where(turn < visits[0, 0], jnp.clip(doc_length[0] - shard * size, 0, size), 0)

    low = [0] + [j & -j for j in range(1, n_keys)]
    chips = range(2, n_keys, 2)

    cache = {0: cache_own}
    for j in list(chips) + list(range(1, n_keys, 2)):
        cache[j] = swap(cache[j ^ low[j]], low[j])

    column = [copies]
    for d in range(1, n_qry):
        column.append(lax.ppermute(copies, "qry", [(peer(i, d, n_qry), i) for i in range(n_qry)]))
    slots = {0: jnp.concatenate(column, axis=0)}
    for j in chips:
        slots[j] = swap(slots[j ^ low[j]], low[j])
    other = [swap(slots[j], 1) for j in range(0, n_keys, 2)]
    slots = [slots[j] for j in range(0, n_keys, 2)]

    stages = [("own", [0]), ("partner", [1]), ("chip", list(chips)), ("far", list(range(3, n_keys, 2)))]
    stages = [stage for stage in stages if stage[1]]
    state = None
    for name, offsets in stages:
        last = name == stages[-1][0]
        state = teacher(live, flat, [(j, cache[j]) for j in offsets], state, last, scale)
    teacher_rows, teacher_turned = state

    away, prob, cast, diff, inner, values = student(flat, teacher_turned, slots, other, per, half, scale)
    own, teacher_out = own_half(flat, teacher_rows, prob, cast, diff, inner, values, half, scale)
    sent = packed(own, away, swap(away, 1), per)

    groups = [[(2 * x + c) * n_qry + q for x in range(n_chip) for q in range(n_qry)] for c in range(2)]
    heard = lax.all_to_all(sent, ("keys", "qry"), 0, 0, axis_index_groups=groups, tiled=True)
    slot_grad, new_params, new_first, new_second, loss = update(
        heard, slot_params, first_moment, second_moment, rows * n_keys * n_qry
    )
    teacher_out = teacher_out.reshape(tok, heads, width)
    return (teacher_out, slot_grad, new_params, new_first, new_second, loss[0, :1])


def solution(mesh):
    return jax.shard_map(
        body,
        mesh=mesh,
        in_specs=(
            P(("grp", "keys", "qry"), None, None),
            P(("grp", "keys"), None),
            P(("grp", "keys"), None),
            P(("grp", "keys"), "qry"),
            P(("grp", "keys"), "qry"),
            P("grp"),
            P(("grp", "keys", "qry"), None),
            P(("grp", "keys", "qry"), None),
            P(("grp", "keys", "qry"), None),
        ),
        out_specs=(
            P(("grp", "keys", "qry"), None, None),
            P(("grp", "keys", "qry"), None),
            P(("grp", "keys", "qry"), None),
            P(("grp", "keys", "qry"), None),
            P(("grp", "keys", "qry"), None),
            P("grp"),
        ),
        check_vma=False,
    )
```

```python
import math

import jax
import jax.numpy as jnp
from jax import lax
from jax.experimental import pallas as pl
from jax.experimental.pallas import tpu as pltpu
from jax.sharding import PartitionSpec as P


NEG = -1e30
PAD = 8
LANES = 128
TILE = 128
GRANT = 24 * 2**20


def nt(left, right):
    return lax.dot_general(left, right, (((1,), (1,)), ((), ())), preferred_element_type=jnp.float32)


def nn(left, right):
    return jnp.dot(left, right, preferred_element_type=jnp.float32)


def with_ones(values):
    turned = values.T
    return jnp.concatenate([turned, jnp.ones((PAD, turned.shape[1]), turned.dtype)], axis=0)


def fold(block, join):
    groups = [block[r:r + PAD] for r in range(0, block.shape[0], PAD)]
    while len(groups) > 1:
        groups = [join(*groups[g:g + 2]) if g + 1 < len(groups) else groups[g] for g in range(0, len(groups), 2)]
    return groups[0]


def peer(index, d, count):
    if count & (count - 1):
        return (index - d + count) % count if isinstance(index, int) else lax.rem(index - d + count, count)
    return index ^ d


def row_block(rows):
    return math.gcd(rows, 256)


def call(kernel, out, arrays, scratch=(), hbm_out=()):
    vm, hbm = pl.BlockSpec(memory_space=pltpu.VMEM), pl.BlockSpec(memory_space=pltpu.HBM)
    arrays = [pltpu.with_memory_space_constraint(a, pltpu.VMEM) for a in arrays]
    spaces = [pltpu.HBM if i in hbm_out else pltpu.VMEM for i in range(len(out))]
    return pl.pallas_call(
        kernel,
        out_shape=tuple(space(s, d) for space, (s, d) in zip(spaces, out)),
        in_specs=[vm] * len(arrays),
        out_specs=tuple(hbm if i in hbm_out else vm for i in range(len(out))),
        scratch_shapes=list(scratch),
        compiler_params=pltpu.CompilerParams(vmem_limit_bytes=GRANT),
    )(*arrays)


def load(queries, keys, values, slot_params):
    size, width = keys.shape
    ins = [pltpu.with_memory_space_constraint(a, pltpu.HBM) for a in (slot_params, keys, values, queries)]

    per = slot_params.shape[0]

    def kernel(*refs):
        sources, (slots_ref, cache_ref, q_ref, full_ref, sems) = refs[:4], refs[4:]
        targets = (full_ref, cache_ref.at[pl.ds(0, size)], cache_ref.at[pl.ds(size, size)], q_ref)
        moves = [pltpu.make_async_copy(a, b, sems.at[i]) for i, (a, b) in enumerate(zip(sources, targets))]
        for move in moves:
            move.start()
        moves[0].wait()
        slots = full_ref[...].astype(jnp.bfloat16)
        slots_ref[...] = slots
        cache_ref[2 * size:2 * size + per, :] = slots[:, :width]
        cache_ref[2 * size + per:, :] = slots[:, width:]
        for move in moves[1:]:
            move.wait()

    return pl.pallas_call(
        kernel,
        out_shape=(
            pltpu.VMEM(slot_params.shape, jnp.bfloat16),
            pltpu.VMEM((2 * (size + per), width), keys.dtype),
            pltpu.VMEM(queries.shape, queries.dtype),
        ),
        in_specs=[pl.BlockSpec(memory_space=pltpu.HBM)] * 4,
        out_specs=(pl.BlockSpec(memory_space=pltpu.VMEM),) * 3,
        scratch_shapes=[
            pltpu.VMEM(slot_params.shape, slot_params.dtype),
            pltpu.SemaphoreType.DMA((4,)),
        ],
        compiler_params=pltpu.CompilerParams(vmem_limit_bytes=GRANT),
        name="load",
    )(*ins)


def teacher(live, queries, segments, size, state, last, scale):
    rows, width = queries.shape
    step = row_block(rows)
    shapes = [((1, rows), jnp.float32), ((width + PAD, rows), jnp.float32)]
    ends = [((rows, width), jnp.bfloat16), ((width, rows), jnp.bfloat16)]
    offsets = [j for j, _ in segments]
    first = state is None
    factor = scale * math.log2(math.e)

    def kernel(live_ref, q_ref, *refs):
        seg, refs = refs[: len(offsets)], refs[len(offsets):]
        if not first:
            (big_in, acc_in), refs = refs[:2], refs[2:]
        if last:
            (out_ref, outt_ref), refs = refs[:2], refs[2:]
        big_ref, acc_ref, score_ref, peak_ref = refs
        if first:
            big_ref[...] = jnp.full(big_ref.shape, NEG, jnp.float32)
            acc_ref[...] = jnp.zeros(acc_ref.shape, jnp.float32)
        else:
            big_ref[...] = big_in[...]
            acc_ref[...] = acc_in[...]
        blocks = [pl.ds(at, step) for at in range(0, rows, step)]
        for s, offset in enumerate(offsets):
            cache_ref = seg[s]
            tile = math.gcd(size, TILE)
            count = jnp.max(live_ref[offset:offset + 1, :])

            @pl.when(count > 0)
            def _():
                live = lax.broadcasted_iota(jnp.int32, (size, width), 0) < count
                keys = jnp.where(live, cache_ref[:size, :], cache_ref[:1, :])
                turned = with_ones(cache_ref[size:2 * size, :])
                turned = jnp.where(
                    lax.broadcasted_iota(jnp.int32, turned.shape, 1) < count, turned, jnp.zeros_like(turned)
                )
                for at in blocks:
                    peak = jnp.full((PAD, step), NEG, jnp.float32)
                    for t in range(0, size, tile):
                        score = nt(keys[t:t + tile], q_ref[at, :])
                        score_ref[t:t + tile, at] = score
                        peak = jnp.maximum(peak, fold(score, jnp.maximum))
                    peak_ref[:, at] = jnp.max(peak, axis=0, keepdims=True)
                for at in blocks:
                    big = big_ref[:, at]
                    new_big = jnp.maximum(big, peak_ref[:, at])
                    weight = jnp.exp2((score_ref[:, at] - new_big) * factor).astype(jnp.bfloat16)
                    fade = jnp.exp2((big - new_big) * factor)
                    acc_ref[:, at] = acc_ref[:, at] * fade + nn(turned, weight)
                    big_ref[:, at] = new_big

        if last:
            for i in range(rows // step):
                at = i * step
                total = acc_ref[width:width + 1, pl.ds(at, step)]
                done = (acc_ref[:width, pl.ds(at, step)] * (1.0 / total)).astype(jnp.bfloat16)
                outt_ref[:, pl.ds(at, step)] = done
                out_ref[pl.ds(at, step), :] = done.T

    arrays = [queries] + [a for _, a in segments] + ([] if first else list(state))
    scratch = [pltpu.VMEM(s, d) for s, d in shapes] if last else []
    scratch += [
        pltpu.VMEM((size, rows), jnp.float32), pltpu.VMEM((1, rows), jnp.float32)
    ]
    return call(kernel, ends if last else shapes, [live] + arrays, scratch)


def gradient_half(start, half, q_ref, prob_ref, cast_ref, diff_ref, inner_ref, values_ref, grad_ref, dscore_ref, scale):
    rows, width = q_ref.shape
    step = row_block(rows)
    values = values_ref[pl.ds(start, half), :]
    for at in range(0, rows, step):
        at = pl.ds(at, step)
        slope = nt(values, diff_ref[at, :]) - inner_ref[:, at]
        dscore_ref[:, at] = (prob_ref[pl.ds(start, half), at] * slope).astype(jnp.bfloat16)
    grad_ref[:half, width:] = nn(cast_ref[pl.ds(start, half), :], diff_ref[...])
    grad_ref[:half, :width] = nn(dscore_ref[...], q_ref[...]) * scale


def student(queries, teach, caches, slots, other, per, half, scale):
    rounds = len(slots)
    n_caches = len(caches)
    rows, width = queries.shape
    step = row_block(rows)
    pieces = slots[0].shape[0] // per
    count = 2 * rounds * (pieces + 1) * per
    tail = caches[0].shape[0] - 2 * per
    tile = math.gcd(count, TILE)
    factor = scale * math.log2(math.e)

    def kernel(q_ref, teach_ref, *refs):
        near, refs = refs[:n_caches], refs[n_caches:]
        sources, refs = refs[: 2 * rounds], refs[2 * rounds:]
        grad_ref, prob_ref, cast_ref, diff_ref, inner_ref, values_ref, keys_ref, dscore_ref = refs
        n_chip, n_qry = lax.axis_size("keys") // 2, lax.axis_size("qry")
        me, mine = lax.axis_index("keys"), lax.axis_index("qry")
        core, chip = lax.rem(me, 2), lax.div(me, 2)

        def put(c, x, index, keys, values):
            to = pl.multiple_of(((c * n_chip + (chip ^ x)) * n_qry + index) * per, per)
            keys_ref[pl.ds(to, per), :] = keys
            values_ref[pl.ds(to, per), :] = values

        for j, source in enumerate(near):
            put(core ^ (j & 1), j // 2, mine, source[tail:tail + per, :], source[tail + per:, :])
        for r, source in enumerate(sources):
            c, x = (core, r) if r < rounds else (1 - core, r - rounds)
            for d in range(pieces):
                piece = source[pl.ds(d * per, per), :]
                put(c, x, peer(mine, d + 1, n_qry), piece[:, :width], piece[:, width:])
        turned = with_ones(values_ref[...])
        squares = jnp.zeros((width, step), jnp.float32)
        blocks = [pl.ds(at, step) for at in range(0, rows, step)]
        for at in blocks:
            peak = jnp.full((PAD, step), NEG, jnp.float32)
            for t in range(0, count, tile):
                score = nt(keys_ref[t:t + tile, :], q_ref[at, :])
                prob_ref[t:t + tile, at] = score
                peak = jnp.maximum(peak, fold(score, jnp.maximum))
            inner_ref[:, at] = jnp.max(peak, axis=0, keepdims=True)
        for at in blocks:
            total = jnp.zeros((PAD, step), jnp.float32)
            for t in range(0, count, tile):
                weight = jnp.exp2((prob_ref[t:t + tile, at] - inner_ref[:, at]) * factor)
                prob_ref[t:t + tile, at] = weight
                total = total + fold(weight, jnp.add)
            inner_ref[:, at] = 1.0 / jnp.sum(total, axis=0, keepdims=True)
        for at in blocks:
            prob = prob_ref[:, at] * inner_ref[:, at]
            prob_ref[:, at] = prob
            cast = prob.astype(jnp.bfloat16)
            cast_ref[:, at] = cast
            both = nn(turned, cast)
            out, mass = both[:width, :], both[width:width + 1, :]
            diff = out - teach_ref[:, at].astype(jnp.float32)
            squares = squares + diff * diff
            short = diff.astype(jnp.bfloat16)
            diff_ref[at, :] = short.T
            inner_ref[:, at] = jnp.sum(short.astype(jnp.float32) * out, axis=0, keepdims=True) / mass
        grad_ref[half:, :] = jnp.full((PAD, 2 * width), jnp.sum(squares), jnp.float32)
        gradient_half(
            pl.multiple_of((1 - core) * half, half),
            half, q_ref, prob_ref, cast_ref, diff_ref, inner_ref, values_ref, grad_ref, dscore_ref, scale,
        )

    return call(
        kernel,
        [
            ((half + PAD, 2 * width), jnp.float32),
            ((count, rows), jnp.float32),
            ((count, rows), jnp.bfloat16),
            ((rows, width), jnp.bfloat16),
            ((1, rows), jnp.float32),
            ((count, width), jnp.bfloat16),
        ],
        [queries, teach, *caches, *slots, *other],
        [pltpu.VMEM((count, width), jnp.bfloat16), pltpu.VMEM((half, rows), jnp.bfloat16)],
    )


def own_half(queries, teach_rows, prob, cast, diff, inner, values, half, scale):
    rows, width = queries.shape

    def kernel(rows_ref, q_ref, prob_ref, cast_ref, diff_ref, inner_ref, values_ref, *refs):
        grad_ref, out_ref, dscore_ref, sem = refs
        write = pltpu.make_async_copy(rows_ref, out_ref, sem)
        write.start()
        start = pl.multiple_of(lax.rem(lax.axis_index("keys"), 2) * half, half)
        gradient_half(
            start, half, q_ref, prob_ref, cast_ref, diff_ref, inner_ref, values_ref, grad_ref, dscore_ref, scale
        )
        write.wait()

    return call(
        kernel, [((half, 2 * width), jnp.float32), ((rows, width), jnp.bfloat16)],
        [teach_rows, queries, prob, cast, diff, inner, values],
        [pltpu.VMEM((half, rows), jnp.bfloat16), pltpu.SemaphoreType.DMA(())], hbm_out=(1,),
    )


def packed(own, away, got, per):
    half, wide = own.shape
    blocks = half // per

    def kernel(own_ref, away_ref, got_ref, out_ref):
        squares = away_ref[half:, :LANES] + got_ref[half:, :LANES]
        one = squares.astype(jnp.bfloat16)
        left = squares - one.astype(jnp.float32)
        two = left.astype(jnp.bfloat16)
        three = (left - two.astype(jnp.float32)).astype(jnp.bfloat16)
        place = lax.broadcasted_iota(jnp.int32, (PAD, LANES), 0)
        zero = jnp.zeros((PAD, LANES), jnp.float32)
        parts = jnp.where(
            place == 0, one.astype(jnp.float32),
            jnp.where(place == 1, two.astype(jnp.float32), jnp.where(place == 2, three.astype(jnp.float32), zero)),
        ).astype(jnp.bfloat16)
        for b in range(blocks):
            at = b * per
            out_ref[b, :per, :] = (own_ref[pl.ds(at, per), :] + got_ref[pl.ds(at, per), :]).astype(jnp.bfloat16)
            for at in range(0, wide, LANES):
                out_ref[b, per:, pl.ds(at, LANES)] = parts

    return call(kernel, [((blocks, per + PAD, wide), jnp.bfloat16)], [own, away, got])[0]


def update(heard, slot_params, first_moment, second_moment, terms):
    per, wide = slot_params.shape

    def kernel(heard_ref, params_ref, first_ref, second_ref, *refs):
        outs, bufs, sems = refs[:5], refs[5:10], refs[10]
        moves = [pltpu.make_async_copy(b, o, sems.at[i]) for i, (b, o) in enumerate(zip(bufs, outs))]
        grad = jnp.zeros((per, wide), jnp.float32)
        tail = jnp.zeros((PAD, LANES), jnp.float32)
        for b in range(heard_ref.shape[0]):
            grad = grad + heard_ref[b, :per, :].astype(jnp.float32)
            tail = tail + heard_ref[b, per:, :LANES].astype(jnp.float32)
        bufs[0][...] = grad
        moves[0].start()
        new_first = 0.9 * first_ref[...] + 0.1 * grad
        bufs[2][...] = new_first
        moves[2].start()
        new_second = 0.95 * second_ref[...] + 0.05 * grad * grad
        bufs[3][...] = new_second
        moves[3].start()
        bufs[4][...] = jnp.sum(tail, axis=0, keepdims=True) / terms
        moves[4].start()
        bufs[1][...] = params_ref[...] - 0.02 * new_first / (jnp.sqrt(new_second) + 1e-08)
        moves[1].start()
        for move in moves:
            move.wait()

    outs = [((per, wide), jnp.float32)] * 4 + [((1, LANES), jnp.float32)]
    return call(
        kernel, outs, [heard, slot_params, first_moment, second_moment],
        [pltpu.VMEM(s, d) for s, d in outs] + [pltpu.SemaphoreType.DMA((5,))], hbm_out=(0, 1, 2, 3, 4),
    )


def body(
    queries,
    cache_keys,
    cache_values,
    entry,
    visits,
    doc_length,
    slot_params,
    first_moment,
    second_moment,
):
    n_keys, n_qry = lax.axis_size("keys"), lax.axis_size("qry")
    tok, heads, width = queries.shape
    rows = tok * heads
    per = slot_params.shape[0]
    n_chip = n_keys // 2
    half = n_chip * n_qry * per
    scale = 1.0 / math.sqrt(width)

    def swap(block, bit):
        return lax.ppermute(block, "keys", [(k, k ^ bit) for k in range(n_keys)])

    copies, cache_own, flat = load(queries.reshape(rows, width), cache_keys, cache_values, slot_params)

    me, size = lax.axis_index("keys"), cache_keys.shape[0]
    shard = me ^ lax.broadcasted_iota(jnp.int32, (-(-n_keys // PAD) * PAD, LANES), 0)
    turn = lax.rem(shard - me - entry[0, 0] + 2 * n_keys, n_keys)
    live = jnp.where(turn < visits[0, 0], jnp.clip(doc_length[0] - shard * size, 0, size), 0)

    low = [0] + [j & -j for j in range(1, n_keys)]
    chips = range(2, n_keys, 2)

    cache = {0: cache_own}
    for j in list(chips) + list(range(1, n_keys, 2)):
        cache[j] = swap(cache[j ^ low[j]], low[j])

    column = []
    for d in range(1, n_qry):
        column.append(lax.ppermute(copies, "qry", [(peer(i, d, n_qry), i) for i in range(n_qry)]))
    slots = {0: jnp.concatenate(column, axis=0)}
    for j in chips:
        slots[j] = swap(slots[j ^ low[j]], low[j])
    other = [swap(slots[j], 1) for j in range(0, n_keys, 2)]
    slots = [slots[j] for j in range(0, n_keys, 2)]

    stages = [("own", [0]), ("partner", [1]), ("chip", list(chips)), ("far", list(range(3, n_keys, 2)))]
    stages = [stage for stage in stages if stage[1]]
    state = None
    for name, offsets in stages:
        last = name == stages[-1][0]
        state = teacher(live, flat, [(j, cache[j]) for j in offsets], cache_keys.shape[0], state, last, scale)
    teacher_rows, teacher_turned = state

    away, prob, cast, diff, inner, values = student(
        flat, teacher_turned, [cache[j] for j in range(n_keys)], slots, other, per, half, scale
    )
    own, teacher_out = own_half(flat, teacher_rows, prob, cast, diff, inner, values, half, scale)
    sent = packed(own, away, swap(away, 1), per)

    groups = [[(2 * x + c) * n_qry + q for x in range(n_chip) for q in range(n_qry)] for c in range(2)]
    heard = lax.all_to_all(sent, ("keys", "qry"), 0, 0, axis_index_groups=groups, tiled=True)
    slot_grad, new_params, new_first, new_second, loss = update(
        heard, slot_params, first_moment, second_moment, rows * n_keys * n_qry
    )
    teacher_out = teacher_out.reshape(tok, heads, width)
    return (teacher_out, slot_grad, new_params, new_first, new_second, loss[0, :1])


def solution(mesh):
    return jax.shard_map(
        body,
        mesh=mesh,
        in_specs=(
            P(("grp", "keys", "qry"), None, None),
            P(("grp", "keys"), None),
            P(("grp", "keys"), None),
            P(("grp", "keys"), "qry"),
            P(("grp", "keys"), "qry"),
            P("grp"),
            P(("grp", "keys", "qry"), None),
            P(("grp", "keys", "qry"), None),
            P(("grp", "keys", "qry"), None),
        ),
        out_specs=(
            P(("grp", "keys", "qry"), None, None),
            P(("grp", "keys", "qry"), None),
            P(("grp", "keys", "qry"), None),
            P(("grp", "keys", "qry"), None),
            P(("grp", "keys", "qry"), None),
            P("grp"),
        ),
        check_vma=False,
    )
```
